256 devices in a mesh: dp: 4 (over x_hi, core), expert: 64 (over x_lo, y, z).
Axes of the slice: x: 4 (x_hi: 2, x_lo: 2; x = x_hi * 2 + x_lo), y: 4, z: 8, core: 2. Of those that a mesh axis runs over, the one named last changes fastest.
Arguments:
- tokens_in: bfloat16 [2, 2048, 2048], P(None, 'expert', 'dp'), may hold values from -6 to 6
- route_ids: int32 [2, 2048, 8], P(None, 'expert'), may hold values from 0 to 127, all different within a row; in each aligned block of 32 rows (0 to 31, 32 to 63, ..., all dimensions but the last counted through in order) at most 4 rows name the same one
- route_gates: float32 [2, 2048, 8], P(None, 'expert'), may hold values from 0.1 to 1
- cotangent: bfloat16 [2, 2048, 2048], P(None, 'expert', 'dp'), may hold values from -0.75 to 0.75
- gate_proj: bfloat16 [128, 1024, 1536], P(None, 'expert', 'dp'), may hold values from -0.125 to 0.125
- up_proj: bfloat16 [128, 1024, 1536], P(None, 'expert', 'dp'), may hold values from -0.125 to 0.125
- down_proj: bfloat16 [128, 1024, 1536], P(None, 'expert', 'dp'), may hold values from -0.21875 to 0.21875
- replica_plan: int32 [2, 64], replicated, may hold values from 0 to 127, as said below
- capacity: int32 [2, 128], replicated, may hold values from 1 to 2, as said below
Outputs:
- y_out: bfloat16 [2, 2048, 2048], P(None, 'expert', 'dp')
- x_grad: bfloat16 [2, 2048, 2048], P(None, 'expert', 'dp')
- gate_grad: bfloat16 [128, 1024, 1536], P(None, 'expert', 'dp')
- up_grad: bfloat16 [128, 1024, 1536], P(None, 'expert', 'dp')
- down_grad: bfloat16 [128, 1024, 1536], P(None, 'expert', 'dp')
The draws below stay inside these ranges and needn't reach their ends.
Inputs may be any that keep to these rules, and one draw needn't show every extreme that they name: `route_ids`: each token names 8 different experts; among the tokens of one micro-batch on one index of the expert axis (an aligned block of 32), no expert is named more than 2 * 2 times. `replica_plan`: an expert may fill the replica slot of several devices, or of none. Some expert has capacity 2 in every micro-batch.
All inputs are finite; a program needn't handle non-finite values.
Results may differ from the reference program's by a relative error of at most 0.012.
Values may be sent and summed in bfloat16 or wider, within the bound.
No kernel may reach another device: no remote copies, remote signals or barrier semaphores. Data moves between devices by JAX's collectives and lax.ppermute only.
A program may use at most 192 MiB of HBM per device.

```python
import math
import jax
import jax.numpy as jnp
import numpy as np
from jax import lax

D = 2048
FF = 768
TOPK = 8
MICRO = 2
TOK_DEV = 32
EXPERTS = 128
CAP = 2
TOKENS = 2048
N_DP = 4
N_EXPERT = 64


def draw_replica_plan(key, part):
    subkeys = jax.random.split(key, 2 * MICRO)
    per_batch = []
    for batch_index in range(MICRO):
        shuffled = jax.random.permutation(subkeys[2 * batch_index], EXPERTS)
        chosen = jax.random.randint(subkeys[2 * batch_index + 1], (EXPERTS // 2,), 0, 8)
        per_batch.append(shuffled[chosen])
    return jnp.stack(per_batch).astype(jnp.int32)


def draw_capacity(key, part):
    first_key, second_key = jax.random.split(key)
    drawn = jax.random.randint(first_key, (MICRO, EXPERTS), max(1, CAP // 2), CAP + 1)
    forced = jax.random.randint(second_key, (MICRO, 1), 0, EXPERTS)
    return jnp.where(jnp.arange(EXPERTS)[None, :] == forced, CAP, drawn).astype(jnp.int32)


def block_levels(own_key, extent, pieces, low, top_value):
    loudness = 1.0
    for position, blocks in pieces:
        steps = jax.random.uniform(jax.random.fold_in(jax.random.fold_in(own_key, 6), position), (blocks,), jnp.float32, low / len(pieces), top_value / len(pieces))
        loudness = loudness * jnp.repeat(jnp.exp(steps), extent[position] // blocks).reshape((-1,) + (1,) * (len(extent) - 1 - position))
    return loudness


def assign_block(key, own, number, rows, amount, top, reach, slope):
    order = jax.random.permutation(key, amount)
    crowded, ordinary = portions_of(amount, rows * top, reach, slope, True), portions_of(amount, rows * top, reach, slope, False)
    places = jnp.arange(amount)

    def named(lengths, rotation):
        used = int((lengths > 0).sum())
        fixed = max(1, used // 4)
        moved = fixed + (places - fixed + rotation * (used - fixed)) % max(1, amount - fixed)
        return jnp.zeros((amount,), jnp.int32).at[order[jnp.where(places < fixed, places, moved)]].set(jnp.asarray(lengths, jnp.int32))

    lengths = jnp.where(number % 4 == 0, named(crowded, number // 4), named(ordinary, number - number // 4 - 1))
    mixed = jax.random.permutation(jax.random.fold_in(own, 3), amount)
    giver, taker = mixed[0:amount // 2 * 2:2], mixed[1:amount // 2 * 2:2]
    room = jnp.minimum(lengths[giver] - 1, reach - lengths[taker]) // 2
    room = jnp.where((giver == order[0]) | (taker == order[0]) | (lengths[taker] == 0), 0, jnp.maximum(room, 0))
    moved = jax.random.randint(jax.random.fold_in(own, 4), (amount // 2,), 0, 1 << 20) % (room + 1)
    lengths = lengths.at[giver].add(-moved).at[taker].add(moved)
    labels = jnp.searchsorted(jnp.cumsum(lengths), jnp.arange(rows * top), side="right").astype(jnp.int32)
    grid = labels.reshape(top, rows).T
    grid = grid[jax.random.permutation(jax.random.fold_in(own, 1), rows)]
    rotation = jax.random.randint(jax.random.fold_in(own, 2), (rows, 1), 0, top)
    return jnp.take_along_axis(grid, (jnp.arange(top)[None, :] + rotation) % top, axis=1)


def portions_of(number_of, total, most, skew, full):
    portions = [(1 << 20) // math.isqrt(standing ** skew) + 1 for standing in range(1, number_of + 1)]
    largest = most if full else min(most, max(-(-total // number_of), total * portions[0] // sum(portions)))
    least = 1 if total - largest >= number_of - 1 else 0
    given, spare = [largest] + [least] * (number_of - 1), total - largest - least * (number_of - 1)
    while spare > 0:
        free = [i for i in range(1, number_of) if given[i] < largest] or [i for i in range(1, number_of) if given[i] < most]
        mass, left = sum([portions[i] for i in free]), spare
        for i in free:
            extra = min(most - given[i], max(1, left * portions[i] // mass), spare)
            given[i] = given[i] + extra
            spare = spare - extra
    return np.array(given)


def noise(rng, extent, width, reach, pieces=(), held_as=jnp.bfloat16):
    values = width * jax.random.normal(rng, extent, jnp.float32)
    if pieces:
        values = values * block_levels(rng, extent, pieces, -0.22, 0.18)
    return jnp.clip(values, -reach, reach).astype(held_as)


def setup_inputs(seed: int = 0) -> dict:
    key_list = jax.random.split(jax.random.key(seed), 10)
    tokens_in = noise(key_list[0], (MICRO, TOKENS, D), 1.0, 6.0, ((1, 64), (2, 4)))
    route_ids_keys = jax.random.split(jax.random.fold_in(key_list[1], 1), MICRO * TOKENS // TOK_DEV)
    route_ids_turns = jax.random.permutation(jax.random.fold_in(key_list[1], 3), MICRO * TOKENS // TOK_DEV)
    route_ids = jax.vmap(lambda own, number: assign_block(jax.random.fold_in(key_list[1], 2), own, number, TOK_DEV, EXPERTS, TOPK, 2 * CAP, 2))(route_ids_keys, route_ids_turns).reshape((MICRO, TOKENS, TOPK))
    route_gates = jnp.clip(0.1 + 0.9 * jax.random.uniform(key_list[2], (MICRO, TOKENS, TOPK), jnp.float32) ** block_levels(key_list[2], (MICRO, TOKENS, TOPK), ((1, 64),), -0.2, 0.2), 0.1, 1.0)
    cotangent = noise(key_list[3], (MICRO, TOKENS, D), 0.125, 0.75, ((1, 64), (2, 4)))
    gate_proj = noise(key_list[4], (EXPERTS, D // 2, 2 * FF), D ** -0.5, 0.125, ((1, 64), (2, 4)))
    up_proj = noise(key_list[5], (EXPERTS, D // 2, 2 * FF), D ** -0.5, 0.125, ((1, 64), (2, 4)))
    down_proj = noise(key_list[6], (EXPERTS, D // 2, 2 * FF), FF ** -0.5, 0.21875, ((1, 64), (2, 4)))
    replica_plan = draw_replica_plan(jax.random.fold_in(key_list[9], 71), 0)
    capacity = draw_capacity(jax.random.fold_in(key_list[9], 71), 0)
    return dict(tokens_in=tokens_in, route_ids=route_ids, route_gates=route_gates, cotangent=cotangent, gate_proj=gate_proj, up_proj=up_proj, down_proj=down_proj, replica_plan=replica_plan, capacity=capacity)


def unpair(weights):
    count = weights.shape[0]
    spread = weights.reshape(count, D // 2, N_DP, 2, FF // N_DP)
    return spread.transpose(0, 1, 3, 2, 4).reshape(count, D, FF)


def pair(weights):
    count = weights.shape[0]
    spread = weights.reshape(count, D // 2, 2, N_DP, FF // N_DP)
    return spread.transpose(0, 1, 3, 2, 4).reshape(count, D // 2, 2 * FF)


def route_targets(batch_ids, batch_plan, batch_caps):
    expert_ids = jnp.arange(EXPERTS, dtype=jnp.int32)
    devices = jnp.arange(N_EXPERT, dtype=jnp.int32)
    hosting = (batch_plan[None, :] == expert_ids[:, None]).astype(jnp.int32)
    ranking = jnp.cumsum(hosting, axis=1)
    copies = 1 + ranking[:, -1]
    copy_ids = jnp.arange(N_EXPERT + 1, dtype=jnp.int32)
    matched = hosting[:, :, None] * (ranking[:, :, None] == copy_ids[None, None, :]).astype(jnp.int32)
    replica_dev = jnp.sum(matched * devices[None, :, None], axis=1)
    home_target = 3 * (expert_ids // 2) + expert_ids % 2
    target_table = jnp.where(copy_ids[None, :] == 0, home_target[:, None], 3 * replica_dev + 2).astype(jnp.int32)
    ids_dev = batch_ids.reshape(N_EXPERT, TOK_DEV * TOPK).astype(jnp.int32)
    token_of = (jnp.arange(TOKENS * TOPK, dtype=jnp.int32) // TOPK).reshape(N_EXPERT, TOK_DEV * TOPK)
    chosen = (token_of % copies[ids_dev]).astype(jnp.int32)
    target = target_table[ids_dev, chosen]
    limits = batch_caps[ids_dev]
    slot_ids = jnp.arange(3 * N_EXPERT, dtype=jnp.int32)
    onehot = (target[:, :, None] == slot_ids[None, None, :]).astype(jnp.int32)
    before = jnp.sum((jnp.cumsum(onehot, axis=1) - onehot) * onehot, axis=2)
    return target, before, before < limits


def expert_pass(rows_x, rows_grad, gate_w, up_w, down_w):
    quarter = FF // N_DP
    pre_gate = jnp.dot(rows_x, gate_w, preferred_element_type=jnp.float32)
    pre_up = jnp.dot(rows_x, up_w, preferred_element_type=jnp.float32)
    logistic = jax.nn.sigmoid(pre_gate)
    swished = pre_gate * logistic
    hidden = (swished * pre_up).astype(jnp.bfloat16)
    hidden_parts = hidden.astype(jnp.float32).reshape(-1, N_DP, quarter)
    down_parts = down_w.astype(jnp.float32).reshape(N_DP, quarter, D)
    partial_value = lax.optimization_barrier(jnp.einsum("rqf,qfd->qrd", hidden_parts, down_parts).astype(jnp.bfloat16))
    out_route = jnp.sum(partial_value.astype(jnp.float32), axis=0).astype(jnp.bfloat16)
    hidden_grad = jnp.dot(rows_grad, down_w.T, preferred_element_type=jnp.float32)
    gate_pre_grad = (hidden_grad * pre_up * logistic * (1.0 + pre_gate * (1.0 - logistic))).astype(jnp.bfloat16)
    up_pre_grad = (hidden_grad * swished).astype(jnp.bfloat16)
    gate_parts = gate_w.astype(jnp.float32).reshape(D, N_DP, quarter)
    up_parts = up_w.astype(jnp.float32).reshape(D, N_DP, quarter)
    gate_terms = jnp.einsum("rqf,dqf->qrd", gate_pre_grad.astype(jnp.float32).reshape(-1, N_DP, quarter), gate_parts)
    up_terms = jnp.einsum("rqf,dqf->qrd", up_pre_grad.astype(jnp.float32).reshape(-1, N_DP, quarter), up_parts)
    input_partial = lax.optimization_barrier((gate_terms + up_terms).astype(jnp.bfloat16))
    in_route = jnp.sum(input_partial.astype(jnp.float32), axis=0).astype(jnp.bfloat16)
    grads = (jnp.dot(rows_x.T, gate_pre_grad, preferred_element_type=jnp.float32),
             jnp.dot(rows_x.T, up_pre_grad, preferred_element_type=jnp.float32),
             jnp.dot(hidden.T, rows_grad, preferred_element_type=jnp.float32))
    return out_route, in_route, grads


def reference(tokens_in, route_ids, route_gates, cotangent, gate_proj, up_proj, down_proj, replica_plan, capacity):
    gate_full = unpair(gate_proj)
    up_full = unpair(up_proj)
    down_full = unpair(down_proj).transpose(0, 2, 1)
    sentinel = MICRO * TOKENS * TOPK
    devices = jnp.arange(N_EXPERT, dtype=jnp.int32)
    route_table = jnp.full((MICRO, 3 * N_EXPERT, N_EXPERT, CAP), sentinel, dtype=jnp.int32)
    for batch_index in range(MICRO):
        target, before, kept_mask = route_targets(route_ids[batch_index], replica_plan[batch_index], capacity[batch_index])
        route_index = (batch_index * TOKENS * TOPK + jnp.arange(TOKENS * TOPK, dtype=jnp.int32)).reshape(N_EXPERT, TOK_DEV * TOPK)
        slot_index = jnp.where(kept_mask, target, 3 * N_EXPERT).astype(jnp.int32)
        source_index = jnp.broadcast_to(devices[:, None], target.shape).astype(jnp.int32)
        place_index = jnp.minimum(before, CAP - 1).astype(jnp.int32)
        route_table = route_table.at[batch_index, slot_index, source_index, place_index].set(route_index.astype(jnp.int32), mode="drop")
    x_rows = jnp.concatenate([tokens_in.reshape(MICRO * TOKENS, D), jnp.zeros((1, D), jnp.bfloat16)], axis=0)
    scaled = route_gates[:, :, :, None] * cotangent[:, :, None, :].astype(jnp.float32)
    grad_rows = jnp.concatenate([scaled.astype(jnp.bfloat16).reshape(sentinel, D), jnp.zeros((1, D), jnp.bfloat16)], axis=0)

    def run_slot(indices, expert):
        token_index = jnp.where(indices < sentinel, indices // TOPK, MICRO * TOKENS).astype(jnp.int32)
        return expert_pass(x_rows[token_index], grad_rows[indices], gate_full[expert], up_full[expert], down_full[expert])

    out_init = jnp.zeros((sentinel, D), jnp.bfloat16)

    def home_step(running, expert):
        out_routes, in_routes = running
        slot_number = (3 * (expert // 2) + expert % 2).astype(jnp.int32)
        indices = route_table[:, slot_number].reshape(-1)
        out_route, in_route, grads = run_slot(indices, expert)
        out_routes = out_routes.at[indices].set(out_route, mode="drop")
        in_routes = in_routes.at[indices].set(in_route, mode="drop")
        return (out_routes, in_routes), tuple(member.astype(jnp.bfloat16) for member in grads)

    (out_routes, in_routes), home_grads = lax.scan(home_step, (out_init, out_init), jnp.arange(EXPERTS, dtype=jnp.int32))
    totals_init = tuple(lax.optimization_barrier(member).astype(jnp.float32) for member in home_grads)

    def replica_step(running, instance):
        out_routes, in_routes, totals = running
        batch_index = (instance // N_EXPERT).astype(jnp.int32)
        device = (instance % N_EXPERT).astype(jnp.int32)
        expert = replica_plan[batch_index, device].astype(jnp.int32)
        indices = route_table[batch_index, 3 * device + 2].reshape(-1)
        out_route, in_route, grads = run_slot(indices, expert)
        out_routes = out_routes.at[indices].set(out_route, mode="drop")
        in_routes = in_routes.at[indices].set(in_route, mode="drop")
        totals = tuple(running_total.at[expert].add(lax.optimization_barrier(member.astype(jnp.bfloat16)).astype(jnp.float32))
                       for running_total, member in zip(totals, grads))
        return (out_routes, in_routes, totals), None

    (out_routes, in_routes, totals), unused = lax.scan(replica_step, (out_routes, in_routes, totals_init),
                                                      jnp.arange(MICRO * N_EXPERT, dtype=jnp.int32))
    gated = route_gates[:, :, :, None] * out_routes.reshape(MICRO, TOKENS, TOPK, D).astype(jnp.float32)
    y_out = jnp.sum(gated, axis=2).astype(jnp.bfloat16)
    x_grad = jnp.sum(in_routes.reshape(MICRO, TOKENS, TOPK, D).astype(jnp.float32), axis=2).astype(jnp.bfloat16)
    gate_out = pair(totals[0].astype(jnp.bfloat16))
    up_out = pair(totals[1].astype(jnp.bfloat16))
    down_out = pair(totals[2].astype(jnp.bfloat16).transpose(0, 2, 1))
    return (y_out, x_grad, gate_out, up_out, down_out)
```

```python
import functools

import jax
import jax.numpy as jnp
from jax import lax
from jax.experimental import pallas as pl
from jax.experimental.pallas import tpu as pltpu
from jax.sharding import Mesh
from jax.sharding import PartitionSpec as P

INTERPRET = False
EXPERT = ("xl", "y", "z")
DP = ("xh", "c")
HOMES = ("xl", "y", "z", "c")
SLOTS = 4
VMEM = pl.BlockSpec(memory_space=pltpu.VMEM)
SMEM = pl.BlockSpec(memory_space=pltpu.SMEM)


def call(kernel, name, in_specs, out_shape, scratch=()):
    return pl.pallas_call(
        kernel,
        name=name,
        in_specs=in_specs,
        out_specs=jax.tree.map(lambda _: VMEM, out_shape),
        out_shape=out_shape,
        scratch_shapes=scratch,
        interpret=INTERPRET,
        compiler_params=pltpu.CompilerParams(vmem_limit_bytes=56 << 20),
    )


def dot(a, b, a_dim, b_dim):
    return lax.dot_general(
        a, b, (((a_dim,), (b_dim,)), ((), ())), preferred_element_type=jnp.float32
    )


def dispatch_kernel(offsets, pick_ref, high_ref, low_ref, own_ref, other_ref, *out_refs):
    micro = pick_ref.shape[0]
    feats = own_ref.shape[-1]
    rows = pick_ref.shape[1] // offsets

    def step(n, carry):
        m, rx = n // 2, n % 2
        at = pl.ds(pl.multiple_of(m * rows, rows), rows)
        for rc, source in enumerate((own_ref, other_ref)):
            x = source[:, rx, 0, m].reshape(-1, feats)
            g = source[:, rx, 1, m].reshape(-1, feats)
            picked = dot(pick_ref[m], x, 1, 0).astype(jnp.bfloat16)
            scaled = dot(high_ref[m], g, 1, 0) + dot(low_ref[m], g, 1, 0)
            scaled = scaled.astype(jnp.bfloat16)
            for o in range(offsets):
                out_refs[o][2 * rc + rx, 0, at] = picked[o * rows : (o + 1) * rows]
                out_refs[o][2 * rc + rx, 1, at] = scaled[o * rows : (o + 1) * rows]
        return carry

    lax.fori_loop(0, 2 * micro, step, 0)


def combine_kernel(offsets, pick_ref, high_ref, low_ref, *refs):
    row_refs, (keep_ref, send_ref) = refs[:offsets], refs[offsets:]
    micro = pick_ref.shape[0]
    rows = pick_ref.shape[1] // offsets
    line, tokens, feats = keep_ref.shape[0], keep_ref.shape[4], keep_ref.shape[5]

    def step(n, carry):
        m, rx = n // 2, n % 2
        at = pl.ds(pl.multiple_of(m * rows, rows), rows)
        for rc, target in enumerate((keep_ref, send_ref)):
            out = jnp.concatenate([r[2 * rc + rx, 0, at] for r in row_refs], axis=0)
            back = jnp.concatenate([r[2 * rc + rx, 1, at] for r in row_refs], axis=0)
            value = dot(high_ref[m], out, 0, 0) + dot(low_ref[m], out, 0, 0)
            grad = dot(pick_ref[m], back, 0, 0)
            shape = (line, tokens, feats)
            target[:, rx, 0, m] = value.reshape(shape).astype(target.dtype)
            target[:, rx, 1, m] = grad.reshape(shape).astype(target.dtype)
        return carry

    lax.fori_loop(0, 2 * micro, step, 0)


def expert_kernel(offsets, quarter_ref, weight_ref, *refs):
    row_refs, refs = refs[:offsets], refs[offsets:]
    grad_ref, refs = refs[0], refs[1:]
    out_refs, refs = refs[:offsets], refs[offsets:]
    w_scr, pre_scr, act_scr = refs
    _, blocks, _, _, pairs, width = weight_ref.shape
    half = width // 2
    depth = blocks * pairs
    rows = row_refs[0].shape[2]

    def swap(lower, upper):
        lane = lax.broadcasted_iota(jnp.int32, lower.shape, 1)
        first = jnp.where(lane < half, lower, pltpu.roll(upper, half, 1))
        second = jnp.where(lane < half, pltpu.roll(lower, half, 1), upper)
        return first, second

    def gather_rows(blk, which):
        return jnp.concatenate([r[blk, which] for r in row_refs], axis=0)

    pre_scr[...] = jnp.zeros_like(pre_scr)

    def first(blk, carry):
        q = quarter_ref[blk]
        x = gather_rows(blk, 0)
        g = gather_rows(blk, 1)
        for k in range(3):
            lower = weight_ref[q, :, 0, k].reshape(depth, width)
            upper = weight_ref[q, :, 1, k].reshape(depth, width)
            even, odd = swap(lower, upper)
            w_scr[k, blk, :depth] = even
            w_scr[k, blk, depth:] = odd
            pre_scr[k] += dot(g if k == 2 else x, w_scr[k, blk], 1, 0)
        return carry

    lax.fori_loop(0, 4, first, 0)
    gate, up, hidden_grad = pre_scr[0], pre_scr[1], pre_scr[2]
    logistic = jax.nn.sigmoid(gate)
    swished = gate * logistic
    act_scr[2] = (swished * up).astype(jnp.bfloat16)
    act_scr[0] = (hidden_grad * up * logistic * (1.0 + gate * (1.0 - logistic))).astype(
        jnp.bfloat16
    )
    act_scr[1] = (hidden_grad * swished).astype(jnp.bfloat16)

    def second(blk, carry):
        q = quarter_ref[blk]
        x = gather_rows(blk, 0)
        g = gather_rows(blk, 1)
        for k in range(3):
            total = dot(g if k == 2 else x, act_scr[k], 0, 0).astype(jnp.bfloat16)
            lower, upper = swap(total[:depth], total[depth:])
            grad_ref[q, :, 0, k] = lower.reshape(blocks, pairs, width)
            grad_ref[q, :, 1, k] = upper.reshape(blocks, pairs, width)
        out = dot(act_scr[2], w_scr[2, blk], 1, 1).astype(jnp.bfloat16)
        back = dot(act_scr[0], w_scr[0, blk], 1, 1) + dot(act_scr[1], w_scr[1, blk], 1, 1)
        back = back.astype(jnp.bfloat16)
        for o in range(offsets):
            out_refs[o][blk, 0] = out[o * rows : (o + 1) * rows]
            out_refs[o][blk, 1] = back[o * rows : (o + 1) * rows]
        return carry

    lax.fori_loop(0, 4, second, 0)


def routing(route_ids, route_gates, expert_ids, replica_plan, capacity):
    line, micro, tokens, _ = route_ids.shape
    offsets = expert_ids.shape[0]
    match = route_ids[:, :, None] == expert_ids[None, None, :, None, None]
    named = jnp.sum(match.astype(jnp.float32), axis=4).transpose(1, 2, 0, 3)
    gates = jnp.sum(jnp.where(match, route_gates[:, :, None], 0.0), axis=4).transpose(1, 2, 0, 3)
    copies = 1 + jnp.sum(
        (replica_plan[:, None, :] == expert_ids[None, :, None]).astype(jnp.int32), axis=2
    )
    all_ids = jnp.arange(capacity.shape[1], dtype=jnp.int32)
    limit = jnp.sum(
        jnp.where(all_ids[None, None, :] == expert_ids[None, :, None], capacity[:, None, :], 0),
        axis=2,
    )
    token_ids = jnp.arange(tokens, dtype=jnp.int32)
    apart = token_ids[None, :] - token_ids[:, None]
    earlier = apart > 0
    rivals = earlier & (apart % copies[:, :, None, None] == 0)
    place = jnp.sum(named[..., None] * rivals[:, :, None].astype(jnp.float32), axis=3)
    count = jnp.sum(named[..., None] * earlier.astype(jnp.float32), axis=3)
    kept = (named > 0) & (place < limit[:, :, None, None].astype(jnp.float32))
    code = jnp.where(kept, count.astype(jnp.int32), -1)
    line_ids = jnp.arange(line, dtype=jnp.int32)
    slot_ids = jnp.arange(SLOTS, dtype=jnp.int32)
    same = line_ids[:, None, None, None] == line_ids[None, None, :, None]
    chosen = (code[:, :, None, None] == slot_ids[None, :, None, None]) & same
    high = lax.reduce_precision(gates, 8, 7)
    low = gates - high
    shape = (micro, offsets * line * SLOTS, line * tokens)

    def spread(values):
        return jnp.where(chosen, values, 0.0).astype(jnp.bfloat16).reshape(shape)

    return spread(1.0), spread(high[:, :, None, None]), spread(low[:, :, None, None])


def shards(
    sizes,
    tokens_in,
    route_ids,
    route_gates,
    cotangent,
    gate_proj,
    up_proj,
    down_proj,
    replica_plan,
    capacity,
):
    nxl, ny, nz = sizes
    micro, tokens, feats = tokens_in.shape
    expert_count, pairs, width = gate_proj.shape
    xh, core = lax.axis_index("xh"), lax.axis_index("c")
    xl, y, z = (lax.axis_index(name) for name in EXPERT)
    steps = [(dx, dy) for dx in range(nxl) for dy in range(ny)]
    offsets = len(steps)
    swap = [(0, 1), (1, 0)]

    weights = jnp.stack([gate_proj, up_proj, down_proj], axis=1)
    weights = lax.all_to_all(weights, HOMES, split_axis=0, concat_axis=0, tiled=True)

    meta = jnp.stack([route_ids.astype(jnp.float32), route_gates])
    meta = lax.all_gather(meta, "z", axis=0)
    lane = jnp.arange(feats, dtype=jnp.int32)
    source = 2 * (lane % (feats // 2)) + lane // (feats // 2)
    halves = (lane[:, None] == source[None, :]).astype(jnp.bfloat16)
    own = jnp.stack([tokens_in, cotangent]).reshape(-1, feats)
    own = jnp.dot(own, halves, preferred_element_type=jnp.float32).astype(jnp.bfloat16)
    across = lax.ppermute(own, "xh", swap)
    line = lax.all_gather(jnp.concatenate([own, across]), "z", axis=0, tiled=True)
    line_shape = (nz, 2, 2, micro, tokens, feats)
    line_other = lax.ppermute(line, "c", swap).reshape(line_shape)
    line = line.reshape(line_shape)

    expert_ids = jnp.stack(
        [((((xl + dx) % nxl) * ny + (y + dy) % ny) * nz + z) * 2 + core for dx, dy in steps]
    )
    selections = routing(
        meta[:, 0].astype(jnp.int32), meta[:, 1], expert_ids, replica_plan, capacity
    )
    chunk_rows = micro * nz * SLOTS
    chunk = jax.ShapeDtypeStruct((4, 2, chunk_rows, feats), jnp.bfloat16)
    sent = call(
        functools.partial(dispatch_kernel, offsets), "dispatch", [VMEM] * 5, (chunk,) * offsets
    )(*selections, line, line_other)

    def moved(pieces, sign):
        done = [pieces[0]]
        for (dx, dy), piece in list(zip(steps, pieces))[1:]:
            pairs_list = [
                (a * ny + b, ((a + sign * dx) % nxl) * ny + (b + sign * dy) % ny)
                for a in range(nxl)
                for b in range(ny)
            ]
            done.append(lax.ppermute(piece, ("xl", "y"), pairs_list))
        return done

    arrived = moved(sent, 1)
    blk = jnp.arange(4, dtype=jnp.int32)
    quarters = (xh ^ (blk % 2)) * 2 + (core ^ (blk // 2))
    rows_all = offsets * chunk_rows
    view = (4, expert_count // 8, 2, 3, pairs, width)
    results = call(
        functools.partial(expert_kernel, offsets),
        "expert",
        [SMEM] + [VMEM] * (1 + offsets),
        (jax.ShapeDtypeStruct(view, jnp.bfloat16),) + (chunk,) * offsets,
        scratch=(
            pltpu.VMEM((3, 4, feats, width), jnp.bfloat16),
            pltpu.VMEM((3, rows_all, width), jnp.float32),
            pltpu.VMEM((3, rows_all, width), jnp.bfloat16),
        ),
    )(quarters, weights.reshape(view), *arrived)
    grads = results[0].reshape(expert_count, 3, pairs, width)
    grads = lax.all_to_all(grads, HOMES, split_axis=0, concat_axis=0, tiled=True)

    returned = moved(results[1:], -1)
    keep, send = call(
        functools.partial(combine_kernel, offsets),
        "combine",
        [VMEM] * (3 + offsets),
        (
            jax.ShapeDtypeStruct(line_shape, jnp.float32),
            jax.ShapeDtypeStruct(line_shape, jnp.bfloat16),
        ),
    )(*selections, *returned)
    keep = (keep + lax.ppermute(send, "c", swap).astype(jnp.float32)).astype(jnp.bfloat16)
    keep = lax.psum_scatter(keep.reshape(-1, feats), "z", scatter_dimension=0, tiled=True)
    keep = keep.reshape(2, -1, feats)
    total = keep[0].astype(jnp.float32) + lax.ppermute(keep[1], "xh", swap).astype(jnp.float32)
    total = jnp.dot(total.astype(jnp.bfloat16), halves.T, preferred_element_type=jnp.float32)
    total = total.astype(jnp.bfloat16).reshape(2, micro, tokens, feats)
    return (total[0], total[1], grads[:, 0], grads[:, 1], grads[:, 2])


def build(devices, sizes):
    mesh = Mesh(devices.reshape((2, 2) + sizes), DP + EXPERT)
    weight = P(None, EXPERT, DP)
    in_specs = (weight, P(None, EXPERT), P(None, EXPERT), weight, weight, weight, weight, P(), P())
    return jax.shard_map(
        functools.partial(shards, sizes),
        mesh=mesh,
        in_specs=in_specs,
        out_specs=(weight,) * 5,
        check_vma=False,
    )


def solution(mesh):
    return build(mesh.devices, (2, 4, 8))
```

```python
import functools

import jax
import jax.numpy as jnp
from jax import lax
from jax.experimental import pallas as pl
from jax.experimental.pallas import tpu as pltpu
from jax.sharding import Mesh
from jax.sharding import PartitionSpec as P


INTERPRET = False
EXPERT = ("xl", "y", "z")
DP = ("xh", "c")
HOMES = ("xl", "y", "z", "c")
SLOTS = 4
VMEM = pl.BlockSpec(memory_space=pltpu.VMEM)
SMEM = pl.BlockSpec(memory_space=pltpu.SMEM)


def call(kernel, in_specs, out_shape, scratch=()):
    return pl.pallas_call(
        kernel,
        in_specs=in_specs,
        out_specs=jax.tree.map(lambda _: VMEM, out_shape),
        out_shape=out_shape,
        scratch_shapes=scratch,
        interpret=INTERPRET,
        compiler_params=pltpu.CompilerParams(vmem_limit_bytes=56 << 20),
    )


def dot(a, b, a_dim, b_dim):
    return lax.dot_general(
        a, b, (((a_dim,), (b_dim,)), ((), ())), preferred_element_type=jnp.float32
    )


def dispatch_kernel(offsets, tokens, pick_ref, high_ref, low_ref, own_ref, other_ref, *out_refs):
    micro = pick_ref.shape[0]
    part = own_ref.shape[-1] // 2
    rows = pick_ref.shape[1] // offsets

    def step(n, carry):
        m, rx, lanes = n // 4, n // 2 % 2, pl.ds(pl.multiple_of(n % 2 * part, part), part)
        at = pl.ds(pl.multiple_of(m * rows, rows), rows)
        from_x = pl.ds(pl.multiple_of((2 * rx * micro + m) * tokens, tokens), tokens)
        from_g = pl.ds(pl.multiple_of(((2 * rx + 1) * micro + m) * tokens, tokens), tokens)
        for rc, source in enumerate((own_ref, other_ref)):
            x = source[:, from_x, lanes].reshape(-1, part)
            g = source[:, from_g, lanes].reshape(-1, part)
            picked = dot(pick_ref[m], x, 1, 0).astype(jnp.bfloat16)
            scaled = dot(high_ref[m], g, 1, 0) + dot(low_ref[m], g, 1, 0)
            scaled = scaled.astype(jnp.bfloat16)
            for o in range(offsets):
                out_refs[o][2 * rc + rx, 0, at, lanes] = picked[o * rows : (o + 1) * rows]
                out_refs[o][2 * rc + rx, 1, at, lanes] = scaled[o * rows : (o + 1) * rows]
        return carry

    lax.fori_loop(0, 4 * micro, step, 0)


def combine_kernel(offsets, pick_ref, high_ref, low_ref, *refs):
    row_refs, (keep_ref, send_ref) = refs[:offsets], refs[offsets:]
    micro = pick_ref.shape[0]
    rows = pick_ref.shape[1] // offsets
    line, tokens, part = keep_ref.shape[0], keep_ref.shape[4], keep_ref.shape[5] // 2

    def step(n, carry):
        m, rx, lanes = n // 4, n // 2 % 2, pl.ds(pl.multiple_of(n % 2 * part, part), part)
        at = pl.ds(pl.multiple_of(m * rows, rows), rows)
        for rc, target in enumerate((keep_ref, send_ref)):
            out = jnp.concatenate([r[2 * rc + rx, 0, at, lanes] for r in row_refs], axis=0)
            back = jnp.concatenate([r[2 * rc + rx, 1, at, lanes] for r in row_refs], axis=0)
            value = dot(high_ref[m], out, 0, 0) + dot(low_ref[m], out, 0, 0)
            grad = dot(pick_ref[m], back, 0, 0)
            shape = (line, tokens, part)
            target[:, rx, 0, m, :, lanes] = value.reshape(shape).astype(target.dtype)
            target[:, rx, 1, m, :, lanes] = grad.reshape(shape).astype(target.dtype)
        return carry

    lax.fori_loop(0, 4 * micro, step, 0)


def swap_halves(lower, upper):
    half = lower.shape[1] // 2
    lane = lax.broadcasted_iota(jnp.int32, lower.shape, 1)
    first = jnp.where(lane < half, lower, pltpu.roll(upper, half, 1))
    second = jnp.where(lane < half, pltpu.roll(lower, half, 1), upper)
    return first, second


def expert_kernel(offsets, quarter_ref, fused_ref, down_ref, *refs):
    row_refs, refs = refs[:offsets], refs[offsets:]
    act_ref, refs = refs[0], refs[1:]
    out_refs, (w_scr, pre_scr) = refs[:offsets], refs[offsets:]
    _, blocks, _, pairs, width = down_ref.shape
    depth = blocks * pairs
    rows = row_refs[0].shape[2]
    pre_scr[...] = jnp.zeros_like(pre_scr)

    def first(blk, carry):
        q = quarter_ref[blk]
        x = jnp.concatenate([r[blk, 0] for r in row_refs], axis=0)
        g = jnp.concatenate([r[blk, 1] for r in row_refs], axis=0)

        def unpack(k, lower, upper, source):
            even, odd = swap_halves(lower.reshape(depth, width), upper.reshape(depth, width))
            w_scr[k, blk, :depth] = even
            w_scr[k, blk, depth:] = odd
            pre_scr[k] += dot(source, w_scr[k, blk], 1, 0)

        def ahead(k, carry):
            unpack(k, fused_ref[q, :, 0, k], fused_ref[q, :, 1, k], x)
            return carry

        lax.fori_loop(0, 2, ahead, 0)
        unpack(2, down_ref[q, :, 0], down_ref[q, :, 1], g)
        return carry

    lax.fori_loop(0, 4, first, 0)
    gate, up, hidden_grad = pre_scr[0], pre_scr[1], pre_scr[2]
    logistic = jax.nn.sigmoid(gate)
    swished = gate * logistic
    act_ref[2] = (swished * up).astype(jnp.bfloat16)
    act_ref[0] = (hidden_grad * up * logistic * (1.0 + gate * (1.0 - logistic))).astype(
        jnp.bfloat16
    )
    act_ref[1] = (hidden_grad * swished).astype(jnp.bfloat16)

    def second(n, carry):
        blk, lanes = n // 2, pl.ds(pl.multiple_of(n % 2 * depth, depth), depth)
        out = dot(act_ref[2], w_scr[2, blk, lanes], 1, 1).astype(jnp.bfloat16)
        back = dot(act_ref[0], w_scr[0, blk, lanes], 1, 1)
        back = (back + dot(act_ref[1], w_scr[1, blk, lanes], 1, 1)).astype(jnp.bfloat16)
        for o in range(offsets):
            out_refs[o][blk, 0, :, lanes] = out[o * rows : (o + 1) * rows]
            out_refs[o][blk, 1, :, lanes] = back[o * rows : (o + 1) * rows]
        return carry

    lax.fori_loop(0, 8, second, 0)


def gradient_kernel(offsets, quarter_ref, act_ref, *refs):
    row_refs, grad_ref = refs[:offsets], refs[offsets]
    _, blocks, _, _, pairs, width = grad_ref.shape
    depth = blocks * pairs

    def step(n, carry):
        blk, k = n // 3, n % 3
        q = quarter_ref[blk]
        source = jnp.concatenate([r[blk, k // 2] for r in row_refs], axis=0)
        total = dot(source, act_ref[k], 0, 0).astype(jnp.bfloat16)
        lower, upper = swap_halves(total[:depth], total[depth:])
        grad_ref[q, :, 0, k] = lower.reshape(blocks, pairs, width)
        grad_ref[q, :, 1, k] = upper.reshape(blocks, pairs, width)
        return carry

    lax.fori_loop(0, 12, step, 0)


def routing(route_ids, high, low, expert_ids, replica_plan, capacity):
    line, micro, _, tokens = route_ids.shape
    offsets = expert_ids.shape[0]
    match = route_ids[:, :, None] == expert_ids[None, None, :, None, None]

    def of_expert(values):
        picked = jnp.where(match, values[:, :, None], 0.0)
        return jnp.sum(picked, axis=3).transpose(1, 2, 0, 3)

    named = of_expert(jnp.ones_like(high))
    copies = 1 + jnp.sum(
        (replica_plan[:, None, :] == expert_ids[None, :, None]).astype(jnp.int32), axis=2
    )
    all_ids = jnp.arange(capacity.shape[1], dtype=jnp.int32)
    limit = jnp.sum(
        jnp.where(all_ids[None, None, :] == expert_ids[None, :, None], capacity[:, None, :], 0),
        axis=2,
    )
    token_ids = jnp.arange(tokens, dtype=jnp.int32)
    apart = token_ids[None, :] - token_ids[:, None]
    earlier = apart > 0
    rivals = earlier & (apart % copies[:, :, None, None] == 0)
    place = jnp.sum(named[..., None] * rivals[:, :, None].astype(jnp.float32), axis=3)
    count = jnp.sum(named[..., None] * earlier.astype(jnp.float32), axis=3)
    kept = (named > 0) & (place < limit[:, :, None, None].astype(jnp.float32))
    code = jnp.where(kept, count.astype(jnp.int32), -1)
    line_ids = jnp.arange(line, dtype=jnp.int32)
    slot_ids = jnp.arange(SLOTS, dtype=jnp.int32)
    same = line_ids[:, None, None, None] == line_ids[None, None, :, None]
    chosen = (code[:, :, None, None] == slot_ids[None, :, None, None]) & same
    shape = (micro, offsets * line * SLOTS, line * tokens)

    def spread(values):
        return jnp.where(chosen, values, 0.0).astype(jnp.bfloat16).reshape(shape)

    high, low = of_expert(high), of_expert(low)
    return spread(1.0), spread(high[:, :, None, None]), spread(low[:, :, None, None])


def shards(
    sizes,
    tokens_in,
    route_ids,
    route_gates,
    cotangent,
    gate_proj,
    up_proj,
    down_proj,
    replica_plan,
    capacity,
):
    nxl, ny, nz = sizes
    micro, tokens, feats = tokens_in.shape
    expert_count, pairs, width = gate_proj.shape
    xh, core = lax.axis_index("xh"), lax.axis_index("c")
    xl, y, z = (lax.axis_index(name) for name in EXPERT)
    steps = [(dx, dy) for dx in range(nxl) for dy in range(ny)]
    offsets = len(steps)
    swap = [(0, 1), (1, 0)]

    def to_homes(blocks):
        return lax.all_to_all(blocks, HOMES, split_axis=0, concat_axis=0, tiled=True)

    lane = jnp.arange(feats, dtype=jnp.int32)
    source = 2 * (lane % (feats // 2)) + lane // (feats // 2)
    halves = (lane[:, None] == source[None, :]).astype(jnp.bfloat16)
    own = jnp.stack([tokens_in, cotangent]).reshape(-1, feats)
    own = jnp.dot(own, halves, preferred_element_type=jnp.float32).astype(jnp.bfloat16)
    high = lax.reduce_precision(route_gates, 8, 7)
    meta = jnp.stack([route_ids.astype(jnp.float32), high, route_gates - high])
    meta = meta.transpose(0, 1, 3, 2).reshape(3, -1).astype(jnp.bfloat16)
    routes = meta.shape[1]
    meta = jnp.pad(meta, ((0, 13), (0, feats - routes)))
    across = lax.ppermute(own, "xh", swap)
    down = to_homes(down_proj)
    fused = to_homes(jnp.stack([gate_proj, up_proj], axis=1))
    line = lax.all_gather(jnp.concatenate([own, across, meta]), "z", axis=0)
    line_other = lax.ppermute(line, "c", swap)
    line_shape = (nz, 2, 2, micro, tokens, feats)

    expert_ids = jnp.stack(
        [((((xl + dx) % nxl) * ny + (y + dy) % ny) * nz + z) * 2 + core for dx, dy in steps]
    )
    start = 2 * own.shape[0]
    meta = line[:, start : start + 3, :routes].reshape(nz, 3, micro, -1, tokens)
    meta = meta.astype(jnp.float32)
    selections = routing(
        meta[:, 0].astype(jnp.int32), meta[:, 1], meta[:, 2], expert_ids, replica_plan, capacity
    )
    chunk_rows = micro * nz * SLOTS
    chunk = jax.ShapeDtypeStruct((4, 2, chunk_rows, feats), jnp.bfloat16)
    sent = call(
        functools.partial(dispatch_kernel, offsets, tokens), [VMEM] * 5, (chunk,) * offsets
    )(*selections, line, line_other)

    def moved(pieces, sign):
        done = [pieces[0]]
        for (dx, dy), piece in list(zip(steps, pieces))[1:]:
            pairs_list = [
                (a * ny + b, ((a + sign * dx) % nxl) * ny + (b + sign * dy) % ny)
                for a in range(nxl)
                for b in range(ny)
            ]
            done.append(lax.ppermute(piece, ("xl", "y"), pairs_list))
        return done

    arrived = moved(sent, 1)
    blk = jnp.arange(4, dtype=jnp.int32)
    quarters = (xh ^ (blk % 2)) * 2 + (core ^ (blk // 2))
    rows_all = offsets * chunk_rows
    view = (4, expert_count // 8, 2)
    act = jax.ShapeDtypeStruct((3, rows_all, width), jnp.bfloat16)
    results = call(
        functools.partial(expert_kernel, offsets),
        [SMEM] + [VMEM] * (2 + offsets),
        (act,) + (chunk,) * offsets,
        scratch=(
            pltpu.VMEM((3, 4, feats, width), jnp.bfloat16),
            pltpu.VMEM((3, rows_all, width), jnp.float32),
        ),
    )(
        quarters,
        fused.reshape(view + (2, pairs, width)),
        down.reshape(view + (pairs, width)),
        *arrived,
    )
    returned = moved(results[1:], -1)
    grads = call(
        functools.partial(gradient_kernel, offsets),
        [SMEM] + [VMEM] * (1 + offsets),
        jax.ShapeDtypeStruct(view + (3, pairs, width), jnp.bfloat16),
    )(quarters, results[0], *arrived)
    grads = to_homes(grads.reshape(expert_count, 3, pairs, width))

    keep, send = call(
        functools.partial(combine_kernel, offsets),
        [VMEM] * (3 + offsets),
        (
            jax.ShapeDtypeStruct(line_shape, jnp.bfloat16),
            jax.ShapeDtypeStruct(line_shape, jnp.bfloat16),
        ),
    )(*selections, *returned)
    send = lax.ppermute(send, "c", swap)
    keep = (keep.astype(jnp.float32) + send.astype(jnp.float32)).astype(jnp.bfloat16)
    keep = lax.psum_scatter(keep.reshape(-1, feats), "z", scatter_dimension=0, tiled=True)
    keep = keep.reshape(2, -1, feats)
    total = keep[0].astype(jnp.float32) + lax.ppermute(keep[1], "xh", swap).astype(jnp.float32)
    total = jnp.dot(total.astype(jnp.bfloat16), halves.T, preferred_element_type=jnp.float32)
    total = total.astype(jnp.bfloat16).reshape(2, micro, tokens, feats)
    return (total[0], total[1], grads[:, 0], grads[:, 1], grads[:, 2])


def build(devices, sizes):
    mesh = Mesh(devices.reshape((2, 2) + sizes), DP + EXPERT)
    weight = P(None, EXPERT, DP)
    in_specs = (weight, P(None, EXPERT), P(None, EXPERT), weight, weight, weight, weight, P(), P())

    def step(*args):
        return shards(sizes, *args)

    return jax.shard_map(
        step,
        mesh=mesh,
        in_specs=in_specs,
        out_specs=(weight,) * 5,
        check_vma=False,
    )


def solution(mesh):
    sizes = (2, 4, 8)
    step = build(mesh.devices, sizes)
    return step
```

```python
import functools

import jax
import jax.numpy as jnp
from jax import lax
from jax.experimental import pallas as pl
from jax.experimental.pallas import tpu as pltpu
from jax.sharding import Mesh
from jax.sharding import PartitionSpec as P


INTERPRET = False
EXPERT = ("xl", "y", "z")
DP = ("xh", "c")
HOMES = ("xl", "y", "z", "c")
SLOTS = 4
META_ROWS = 32


def spec(shape, at=None):
    rank = len(shape)
    if at is None:
        return pl.BlockSpec(shape, lambda i, *refs: (0,) * rank)
    return pl.BlockSpec(shape, lambda i, *refs: (at(i, *refs) + (0,) * rank)[:rank])


def call(kernel, grid, in_specs, out_specs, out_shape, scratch=()):
    return pl.pallas_call(
        kernel,
        grid_spec=pltpu.PrefetchScalarGridSpec(
            num_scalar_prefetch=1,
            grid=(grid,),
            in_specs=in_specs,
            out_specs=out_specs,
            scratch_shapes=scratch,
        ),
        out_shape=out_shape,
        interpret=INTERPRET,
        compiler_params=pltpu.CompilerParams(
            dimension_semantics=("arbitrary",), vmem_limit_bytes=56 << 20
        ),
    )


def dot(a, b, a_dim, b_dim):
    return lax.dot_general(
        a, b, (((a_dim,), (b_dim,)), ((), ())), preferred_element_type=jnp.float32
    )


def select_rows(offsets, tokens, top, expert_ref, meta_ref, divides_ref, limit_ref, pick_refs):
    pick_ref, high_ref, low_ref = pick_refs
    micro = pick_ref.shape[0]
    rows = pick_ref.shape[1] // offsets
    columns = pick_ref.shape[2]
    named_rows = jnp.sum(meta_ref[...].astype(jnp.float32), axis=0)
    token = lax.broadcasted_iota(jnp.int32, (offsets, columns), 1) % tokens
    shape = (offsets * rows, columns)
    row = lax.broadcasted_iota(jnp.int32, shape, 0)
    source = lax.broadcasted_iota(jnp.int32, shape, 1) // tokens
    same = (row % rows) // SLOTS == source
    slot = (row % SLOTS).astype(jnp.float32)

    for m in range(micro):
        at = slice(m * top, (m + 1) * top)
        ids = named_rows[at, :columns]
        gates = (
            named_rows[at, columns : 2 * columns],
            named_rows[(micro + m) * top : (micro + m + 1) * top, :columns],
        )
        named, high, low = [], [], []
        for o in range(offsets):
            match = ids == expert_ref[o].astype(jnp.float32)
            named.append(jnp.sum(match.astype(jnp.float32), axis=0, keepdims=True))
            high.append(jnp.sum(jnp.where(match, gates[0], 0.0), axis=0, keepdims=True))
            low.append(jnp.sum(jnp.where(match, gates[1], 0.0), axis=0, keepdims=True))
        named = jnp.concatenate(named, axis=0)
        count = jnp.zeros_like(named)
        place = jnp.zeros_like(named)
        for apart in range(1, tokens):
            prior = jnp.where(token >= apart, pltpu.roll(named, apart, 1), 0.0)
            count += prior
            place += prior * divides_ref[m, :, apart : apart + 1]
        kept = (named > 0.0) & (place < limit_ref[m, :, :1])
        code = jnp.where(kept, count, -1.0)

        def spread(values):
            pieces = [jnp.broadcast_to(v, (rows, columns)) for v in values]
            return jnp.concatenate(pieces, axis=0)

        chosen = same & (spread([code[o : o + 1] for o in range(offsets)]) == slot)
        pick_ref[m] = jnp.where(chosen, 1.0, 0.0).astype(jnp.bfloat16)
        high_ref[m] = jnp.where(chosen, spread(high), 0.0).astype(jnp.bfloat16)
        low_ref[m] = jnp.where(chosen, spread(low), 0.0).astype(jnp.bfloat16)


def dispatch_kernel(
    offsets, tokens, top, expert_ref, divides_ref, limit_ref, meta_ref, own_ref, other_ref, *refs
):
    pick_refs, out_refs = refs[:3], refs[3:]
    pick_ref, high_ref, low_ref = pick_refs
    micro = pick_ref.shape[0]
    feats = own_ref.shape[2]
    rows = pick_ref.shape[1] // offsets

    @pl.when(pl.program_id(0) == 0)
    def _():
        select_rows(offsets, tokens, top, expert_ref, meta_ref, divides_ref, limit_ref, pick_refs)

    for m in range(micro):
        at = slice(m * rows, (m + 1) * rows)
        for rc, source in enumerate((own_ref, other_ref)):
            x = source[:, m * tokens : (m + 1) * tokens].reshape(-1, feats)
            g = source[:, (micro + m) * tokens : (micro + m + 1) * tokens].reshape(-1, feats)
            picked = dot(pick_ref[m], x, 1, 0).astype(jnp.bfloat16)
            scaled = dot(high_ref[m], g, 1, 0) + dot(low_ref[m], g, 1, 0)
            scaled = scaled.astype(jnp.bfloat16)
            for o in range(offsets):
                out_refs[o][rc, 0, 0, at] = picked[o * rows : (o + 1) * rows]
                out_refs[o][rc, 0, 1, at] = scaled[o * rows : (o + 1) * rows]


def combine_kernel(offsets, expert_ref, pick_ref, high_ref, low_ref, *refs):
    row_refs, (keep_ref, send_ref) = refs[:offsets], refs[offsets:]
    micro = pick_ref.shape[0]
    rows = pick_ref.shape[1] // offsets
    shape = (keep_ref.shape[0],) + keep_ref.shape[4:]
    for m in range(micro):
        at = slice(m * rows, (m + 1) * rows)
        for rc, target in enumerate((keep_ref, send_ref)):
            out = jnp.concatenate([r[rc, 0, 0, at] for r in row_refs], axis=0)
            back = jnp.concatenate([r[rc, 0, 1, at] for r in row_refs], axis=0)
            value = dot(high_ref[m], out, 0, 0) + dot(low_ref[m], out, 0, 0)
            grad = dot(pick_ref[m], back, 0, 0)
            target[:, 0, 0, m] = value.astype(target.dtype).reshape(shape)
            target[:, 0, 1, m] = grad.astype(target.dtype).reshape(shape)


def swap_halves(lower, upper):
    half = lower.shape[1] // 2
    lane = lax.broadcasted_iota(jnp.int32, lower.shape, 1)
    first = jnp.where(lane < half, lower, pltpu.roll(upper, half, 1))
    second = jnp.where(lane < half, pltpu.roll(lower, half, 1), upper)
    return first, second


def expert_kernel(offsets, quarter_ref, fused_ref, down_ref, *refs):
    row_refs, refs = refs[:offsets], refs[offsets:]
    act_ref, refs = refs[0], refs[1:]
    out_refs, (w_scr, pre_scr) = refs[:offsets], refs[offsets:]
    _, blocks, _, pairs, width = down_ref.shape
    depth = blocks * pairs
    rows = row_refs[0].shape[3]
    step = pl.program_id(0)

    @pl.when(step == 0)
    def _():
        pre_scr[...] = jnp.zeros_like(pre_scr)

    @pl.when(step < 4)
    def _():
        x = jnp.concatenate([r[0, 0, 0] for r in row_refs], axis=0)
        g = jnp.concatenate([r[0, 0, 1] for r in row_refs], axis=0)
        for k in range(3):
            if k < 2:
                lower, upper = fused_ref[0, :, 0, k], fused_ref[0, :, 1, k]
            else:
                lower, upper = down_ref[0, :, 0], down_ref[0, :, 1]
            even, odd = swap_halves(lower.reshape(depth, width), upper.reshape(depth, width))
            both = jnp.concatenate([even, odd], axis=0)
            w_scr[k, step] = both
            pre_scr[k] += dot(g if k == 2 else x, both, 1, 0)

    @pl.when(step == 3)
    def _():
        gate, up, hidden_grad = pre_scr[0], pre_scr[1], pre_scr[2]
        logistic = jax.nn.sigmoid(gate)
        swished = gate * logistic
        act_ref[2] = (swished * up).astype(jnp.bfloat16)
        act_ref[0] = (hidden_grad * up * logistic * (1.0 + gate * (1.0 - logistic))).astype(
            jnp.bfloat16
        )
        act_ref[1] = (hidden_grad * swished).astype(jnp.bfloat16)

    @pl.when(step >= 4)
    def _():
        blk = step - 4
        out = dot(act_ref[2], w_scr[2, blk], 1, 1).astype(jnp.bfloat16)
        back = dot(act_ref[0], w_scr[0, blk], 1, 1)
        back = (back + dot(act_ref[1], w_scr[1, blk], 1, 1)).astype(jnp.bfloat16)
        for o in range(offsets):
            out_refs[o][0, 0, 0] = out[o * rows : (o + 1) * rows]
            out_refs[o][0, 0, 1] = back[o * rows : (o + 1) * rows]


def gradient_kernel(offsets, quarter_ref, act_ref, *refs):
    row_refs, grad_ref = refs[:offsets], refs[offsets]
    _, blocks, _, members, pairs, width = grad_ref.shape
    depth = blocks * pairs
    source = jnp.concatenate([r[0, 0, 0] for r in row_refs], axis=0)
    for k in range(members):
        total = dot(source, act_ref[k], 0, 0).astype(jnp.bfloat16)
        lower, upper = swap_halves(total[:depth], total[depth:])
        grad_ref[0, :, 0, k] = lower.reshape(blocks, pairs, width)
        grad_ref[0, :, 1, k] = upper.reshape(blocks, pairs, width)


def shards(
    sizes,
    tokens_in,
    route_ids,
    route_gates,
    cotangent,
    gate_proj,
    up_proj,
    down_proj,
    replica_plan,
    capacity,
):
    nxl, ny, nz = sizes
    micro, tokens, feats = tokens_in.shape
    expert_count, pairs, width = gate_proj.shape
    xh, core = lax.axis_index("xh"), lax.axis_index("c")
    xl, y, z = (lax.axis_index(name) for name in EXPERT)
    steps = [(dx, dy) for dx in range(nxl) for dy in range(ny)]
    offsets = len(steps)
    swap = [(0, 1), (1, 0)]

    def to_homes(blocks):
        return lax.all_to_all(blocks, HOMES, split_axis=0, concat_axis=0, tiled=True)

    lane = jnp.arange(feats, dtype=jnp.int32)
    source = 2 * (lane % (feats // 2)) + lane // (feats // 2)
    halves = (lane[:, None] == source[None, :]).astype(jnp.bfloat16)
    own = jnp.stack([tokens_in, cotangent]).reshape(-1, feats)
    own = jnp.dot(own, halves, preferred_element_type=jnp.float32).astype(jnp.bfloat16)
    columns = nz * tokens
    routes = micro * route_ids.shape[2]
    high = lax.reduce_precision(route_gates, 8, 7)
    meta = jnp.stack([route_ids.astype(jnp.float32), high, route_gates - high])
    meta = meta.transpose(0, 1, 3, 2).astype(jnp.bfloat16).reshape(3, routes, tokens)
    mine = jnp.arange(columns, dtype=jnp.int32) // tokens == z
    meta = jnp.where(mine, jnp.tile(meta, (1, 1, nz)), 0)
    meta = jnp.concatenate(
        [
            jnp.concatenate([meta[0], meta[1]], axis=1),
            jnp.concatenate([meta[2], jnp.zeros_like(meta[2])], axis=1),
        ]
    )
    meta = jnp.pad(meta, ((0, META_ROWS - 2 * routes), (0, feats - 2 * columns)))
    across = lax.ppermute(own, "xh", swap)
    down = to_homes(down_proj)
    fused = to_homes(jnp.stack([gate_proj, up_proj], axis=1))
    line = lax.all_gather(jnp.concatenate([own, across, meta]), "z", axis=0)
    line_other = lax.ppermute(line, "c", swap)
    line_shape = (nz, 2, 2, micro, tokens, feats)

    expert_ids = jnp.stack(
        [((((xl + dx) % nxl) * ny + (y + dy) % ny) * nz + z) * 2 + core for dx, dy in steps]
    )
    copies = 1 + jnp.sum(
        (replica_plan[:, None, :] == expert_ids[None, :, None]).astype(jnp.int32), axis=2
    )
    all_ids = jnp.arange(expert_count, dtype=jnp.int32)
    limit = jnp.sum(
        jnp.where(all_ids[None, None, :] == expert_ids[None, :, None], capacity[:, None, :], 0),
        axis=2,
    )
    apart = jnp.arange(128, dtype=jnp.int32)
    divides = (apart % copies[:, :, None] == 0).astype(jnp.float32)
    limit = jnp.broadcast_to(limit[:, :, None].astype(jnp.float32), divides.shape)
    chunk_rows = micro * nz * SLOTS
    chunk = jax.ShapeDtypeStruct((2, 2, 2, chunk_rows, feats), jnp.bfloat16)
    chunk_pair = spec((2, 1, 2, chunk_rows, feats), lambda i, *refs: (0, i))
    pick_shape = (micro, offsets * nz * SLOTS, columns)
    pick = jax.ShapeDtypeStruct(pick_shape, jnp.bfloat16)
    line_rows = 2 * micro * tokens
    line_spec = spec((nz, line_rows, feats), lambda i, *refs: (0, i))
    sent = call(
        functools.partial(dispatch_kernel, offsets, tokens, route_ids.shape[2]),
        2,
        [spec(divides.shape), spec(limit.shape)]
        + [spec((nz, META_ROWS, feats), lambda i, *refs: (0, 2 * line_rows // META_ROWS))]
        + [line_spec] * 2,
        [spec(pick_shape)] * 3 + [chunk_pair] * offsets,
        [pick] * 3 + [chunk] * offsets,
    )(expert_ids, divides, limit, line, line, line_other)
    selections, sent = sent[:3], sent[3:]

    def moved(pieces, sign):
        done = [pieces[0]]
        for (dx, dy), piece in list(zip(steps, pieces))[1:]:
            pairs_list = [
                (a * ny + b, ((a + sign * dx) % nxl) * ny + (b + sign * dy) % ny)
                for a in range(nxl)
                for b in range(ny)
            ]
            done.append(lax.ppermute(piece, ("xl", "y"), pairs_list))
        return done

    arrived = moved(sent, 1)
    blk = jnp.arange(4, dtype=jnp.int32)
    quarters = (xh ^ (blk % 2)) * 2 + (core ^ (blk // 2))
    rows_all = offsets * chunk_rows
    blocks = expert_count // 8
    view = (4, blocks, 2)
    act = jax.ShapeDtypeStruct((3, rows_all, width), jnp.bfloat16)

    def early(i, *refs):
        i = jnp.minimum(i, 3)
        return (i // 2, i % 2)

    def late(i, *refs):
        i = jnp.maximum(i - 4, 0)
        return (i // 2, i % 2)

    results = call(
        functools.partial(expert_kernel, offsets),
        8,
        [
            spec((1, blocks, 2, 2, pairs, width), lambda i, q: (q[jnp.minimum(i, 3)],)),
            spec((1, blocks, 2, pairs, width), lambda i, q: (q[jnp.minimum(i, 3)],)),
        ]
        + [spec((1, 1, 2, chunk_rows, feats), early)] * offsets,
        [spec(act.shape)] + [spec((1, 1, 2, chunk_rows, feats), late)] * offsets,
        [act] + [chunk] * offsets,
        scratch=(
            pltpu.VMEM((3, 4, feats, width), jnp.bfloat16),
            pltpu.VMEM((3, rows_all, width), jnp.float32),
        ),
    )(
        quarters,
        fused.reshape(view + (2, pairs, width)),
        down.reshape(view + (pairs, width)),
        *arrived,
    )
    returned = moved(results[1:], -1)

    def gradient(which, first, members):
        return call(
            functools.partial(gradient_kernel, offsets),
            4,
            [spec((members, rows_all, width), lambda i, *refs: (first // members,))]
            + [spec((1, 1, 1, chunk_rows, feats), lambda i, *refs: (i // 2, i % 2, which))]
            * offsets,
            spec((1, blocks, 2, members, pairs, width), lambda i, q: (q[i],)),
            jax.ShapeDtypeStruct(view + (members, pairs, width), jnp.bfloat16),
        )(quarters, results[0], *arrived)

    fused_grad = to_homes(gradient(0, 0, 2).reshape(expert_count, 2, pairs, width))
    down_grad = to_homes(gradient(1, 2, 1).reshape(expert_count, pairs, width))

    keep, send = call(
        functools.partial(combine_kernel, offsets),
        2,
        [spec(pick_shape)] * 3 + [chunk_pair] * offsets,
        [spec((nz, 1, 2, micro, tokens, feats), lambda i, *refs: (0, i))] * 2,
        [jax.ShapeDtypeStruct(line_shape, jnp.bfloat16)] * 2,
    )(quarters, *selections, *returned)
    send = lax.ppermute(send, "c", swap)
    keep = (keep.astype(jnp.float32) + send.astype(jnp.float32)).astype(jnp.bfloat16)
    keep = lax.psum_scatter(keep.reshape(-1, feats), "z", scatter_dimension=0, tiled=True)
    keep = keep.reshape(2, -1, feats)
    total = keep[0].astype(jnp.float32) + lax.ppermute(keep[1], "xh", swap).astype(jnp.float32)
    total = jnp.dot(total.astype(jnp.bfloat16), halves.T, preferred_element_type=jnp.float32)
    total = total.astype(jnp.bfloat16).reshape(2, micro, tokens, feats)
    return (total[0], total[1], fused_grad[:, 0], fused_grad[:, 1], down_grad)


def build(devices, sizes):
    mesh = Mesh(devices.reshape((2, 2) + sizes), DP + EXPERT)
    weight = P(None, EXPERT, DP)
    in_specs = (weight, P(None, EXPERT), P(None, EXPERT), weight, weight, weight, weight, P(), P())

    def step(*args):
        return shards(sizes, *args)

    return jax.shard_map(
        step,
        mesh=mesh,
        in_specs=in_specs,
        out_specs=(weight,) * 5,
        check_vma=False,
    )


def solution(mesh):
    sizes = (2, 4, 8)
    step = build(mesh.devices, sizes)
    return step
```

```python
import functools

import jax
import jax.numpy as jnp
from jax import lax
from jax.experimental import pallas as pl
from jax.experimental.pallas import tpu as pltpu
from jax.sharding import Mesh
from jax.sharding import PartitionSpec as P


INTERPRET = False
EXPERT = ("xl", "y", "z")
DP = ("xh", "c")
HOMES = ("xl", "y", "z", "c")
SLOTS = 4
META_ROWS = 32


def spec(shape, at=None):
    rank = len(shape)
    if at is None:
        return pl.BlockSpec(shape, lambda i, *refs: (0,) * rank)
    return pl.BlockSpec(shape, lambda i, *refs: (at(i, *refs) + (0,) * rank)[:rank])


def call(kernel, grid, in_specs, out_specs, out_shape, scratch=()):
    return pl.pallas_call(
        kernel,
        grid_spec=pltpu.PrefetchScalarGridSpec(
            num_scalar_prefetch=1,
            grid=(grid,),
            in_specs=in_specs,
            out_specs=out_specs,
            scratch_shapes=scratch,
        ),
        out_shape=out_shape,
        interpret=INTERPRET,
        compiler_params=pltpu.CompilerParams(
            dimension_semantics=("arbitrary",), vmem_limit_bytes=56 << 20
        ),
    )


def dot(a, b, a_dim, b_dim):
    return lax.dot_general(
        a, b, (((a_dim,), (b_dim,)), ((), ())), preferred_element_type=jnp.float32
    )


def select_rows(offsets, tokens, top, expert_ref, meta_ref, divides_ref, limit_ref, pick_refs):
    pick_ref, high_ref, low_ref = pick_refs
    micro = pick_ref.shape[0]
    rows = pick_ref.shape[1] // offsets
    columns = pick_ref.shape[2]
    named_rows = jnp.sum(meta_ref[...].astype(jnp.float32), axis=0)
    token = lax.broadcasted_iota(jnp.int32, (offsets, columns), 1) % tokens
    shape = (offsets * rows, columns)
    row = lax.broadcasted_iota(jnp.int32, shape, 0)
    source = lax.broadcasted_iota(jnp.int32, shape, 1) // tokens
    same = (row % rows) // SLOTS == source
    slot = (row % SLOTS).astype(jnp.float32)

    for m in range(micro):
        at = slice(m * top, (m + 1) * top)
        ids = named_rows[at, :columns]
        gates = (
            named_rows[at, columns : 2 * columns],
            named_rows[(micro + m) * top : (micro + m + 1) * top, :columns],
        )
        named, high, low = [], [], []
        for o in range(offsets):
            match = ids == expert_ref[o].astype(jnp.float32)
            named.append(jnp.sum(match.astype(jnp.float32), axis=0, keepdims=True))
            high.append(jnp.sum(jnp.where(match, gates[0], 0.0), axis=0, keepdims=True))
            low.append(jnp.sum(jnp.where(match, gates[1], 0.0), axis=0, keepdims=True))
        named = jnp.concatenate(named, axis=0)
        count = jnp.zeros_like(named)
        place = jnp.zeros_like(named)
        for apart in range(1, tokens):
            prior = jnp.where(token >= apart, pltpu.roll(named, apart, 1), 0.0)
            count += prior
            place += prior * divides_ref[m, :, apart : apart + 1]
        kept = (named > 0.0) & (place < limit_ref[m, :, :1])
        code = jnp.where(kept, count, -1.0)

        def spread(values):
            pieces = [jnp.broadcast_to(v, (rows, columns)) for v in values]
            return jnp.concatenate(pieces, axis=0)

        chosen = same & (spread([code[o : o + 1] for o in range(offsets)]) == slot)
        pick_ref[m] = jnp.where(chosen, 1.0, 0.0).astype(jnp.bfloat16)
        high_ref[m] = jnp.where(chosen, spread(high), 0.0).astype(jnp.bfloat16)
        low_ref[m] = jnp.where(chosen, spread(low), 0.0).astype(jnp.bfloat16)


def dispatch_kernel(
    offsets, tokens, top, expert_ref, divides_ref, limit_ref, meta_ref, own_ref, other_ref, *refs
):
    pick_refs, out_refs = refs[:3], refs[3:]
    pick_ref, high_ref, low_ref = pick_refs
    micro = pick_ref.shape[0]
    feats = own_ref.shape[2]
    rows = pick_ref.shape[1] // offsets

    @pl.when(pl.program_id(0) == 0)
    def _():
        select_rows(offsets, tokens, top, expert_ref, meta_ref, divides_ref, limit_ref, pick_refs)

    for m in range(micro):
        at = slice(m * rows, (m + 1) * rows)
        for rc, source in enumerate((own_ref, other_ref)):
            x = source[:, m * tokens : (m + 1) * tokens].reshape(-1, feats)
            g = source[:, (micro + m) * tokens : (micro + m + 1) * tokens].reshape(-1, feats)
            picked = dot(pick_ref[m], x, 1, 0).astype(jnp.bfloat16)
            scaled = dot(high_ref[m], g, 1, 0) + dot(low_ref[m], g, 1, 0)
            scaled = scaled.astype(jnp.bfloat16)
            for o in range(offsets):
                out_refs[o][rc, 0, 0, at] = picked[o * rows : (o + 1) * rows]
                out_refs[o][rc, 0, 1, at] = scaled[o * rows : (o + 1) * rows]


def combine_kernel(offsets, expert_ref, pick_ref, high_ref, low_ref, *refs):
    row_refs, refs = refs[:offsets], refs[offsets:]
    target, added = refs[-1], refs[:-1]
    micro = pick_ref.shape[0]
    rows = pick_ref.shape[1] // offsets
    shape = (target.shape[0],) + target.shape[4:]
    for m in range(micro):
        at = slice(m * rows, (m + 1) * rows)
        out = jnp.concatenate([r[0, 0, 0, at] for r in row_refs], axis=0)
        back = jnp.concatenate([r[0, 0, 1, at] for r in row_refs], axis=0)
        value = (dot(high_ref[m], out, 0, 0) + dot(low_ref[m], out, 0, 0)).reshape(shape)
        grad = dot(pick_ref[m], back, 0, 0).reshape(shape)
        for ref in added:
            value += ref[:, 0, 0, m].astype(jnp.float32)
            grad += ref[:, 0, 1, m].astype(jnp.float32)
        target[:, 0, 0, m] = value.astype(target.dtype)
        target[:, 0, 1, m] = grad.astype(target.dtype)


def swap_halves(lower, upper):
    half = lower.shape[1] // 2
    lane = lax.broadcasted_iota(jnp.int32, lower.shape, 1)
    first = jnp.where(lane < half, lower, pltpu.roll(upper, half, 1))
    second = jnp.where(lane < half, pltpu.roll(lower, half, 1), upper)
    return first, second


def expert_kernel(offsets, quarter_ref, weight_ref, *refs):
    row_refs, refs = refs[:offsets], refs[offsets:]
    grad_ref, refs = refs[0], refs[1:]
    out_refs, (w_scr, row_scr, pre_scr, act_scr) = refs[:offsets], refs[offsets:]
    _, blocks, _, _, pairs, width = weight_ref.shape
    depth = blocks * pairs
    rows = row_refs[0].shape[3]
    step = pl.program_id(0)

    @pl.when(step == 0)
    def _():
        pre_scr[...] = jnp.zeros_like(pre_scr)

    @pl.when(step < 4)
    def _():
        x = jnp.concatenate([r[0, 0, 0] for r in row_refs], axis=0)
        g = jnp.concatenate([r[0, 0, 1] for r in row_refs], axis=0)
        row_scr[step, 0] = x
        row_scr[step, 1] = g
        for k in range(3):
            lower = weight_ref[0, :, 0, k].reshape(depth, width)
            upper = weight_ref[0, :, 1, k].reshape(depth, width)
            both = jnp.concatenate(swap_halves(lower, upper), axis=0)
            w_scr[k, step] = both
            pre_scr[k] += dot(g if k == 2 else x, both, 1, 0)

    @pl.when(step == 3)
    def _():
        gate, up, hidden_grad = pre_scr[0], pre_scr[1], pre_scr[2]
        logistic = jax.nn.sigmoid(gate)
        swished = gate * logistic
        act_scr[2] = (swished * up).astype(jnp.bfloat16)
        act_scr[0] = (hidden_grad * up * logistic * (1.0 + gate * (1.0 - logistic))).astype(
            jnp.bfloat16
        )
        act_scr[1] = (hidden_grad * swished).astype(jnp.bfloat16)

    @pl.when(step >= 4)
    def _():
        blk = step - 4
        for k in range(3):
            total = dot(row_scr[blk, k // 2], act_scr[k], 0, 0).astype(jnp.bfloat16)
            lower, upper = swap_halves(total[:depth], total[depth:])
            grad_ref[0, :, 0, k] = lower.reshape(blocks, pairs, width)
            grad_ref[0, :, 1, k] = upper.reshape(blocks, pairs, width)
        out = dot(act_scr[2], w_scr[2, blk], 1, 1).astype(jnp.bfloat16)
        back = dot(act_scr[0], w_scr[0, blk], 1, 1)
        back = (back + dot(act_scr[1], w_scr[1, blk], 1, 1)).astype(jnp.bfloat16)
        for o in range(offsets):
            out_refs[o][0, 0, 0] = out[o * rows : (o + 1) * rows]
            out_refs[o][0, 0, 1] = back[o * rows : (o + 1) * rows]


def shards(
    sizes,
    tokens_in,
    route_ids,
    route_gates,
    cotangent,
    gate_proj,
    up_proj,
    down_proj,
    replica_plan,
    capacity,
):
    nxl, ny, nz = sizes
    micro, tokens, feats = tokens_in.shape
    expert_count, pairs, width = gate_proj.shape
    xh, core = lax.axis_index("xh"), lax.axis_index("c")
    xl, y, z = (lax.axis_index(name) for name in EXPERT)
    steps = [(dx, dy) for dx in range(nxl) for dy in range(ny)]
    offsets = len(steps)
    swap = [(0, 1), (1, 0)]

    def to_homes(blocks):
        return lax.all_to_all(blocks, HOMES, split_axis=0, concat_axis=0, tiled=True)

    lane = jnp.arange(feats, dtype=jnp.int32)
    source = 2 * (lane % (feats // 2)) + lane // (feats // 2)
    halves = (lane[:, None] == source[None, :]).astype(jnp.bfloat16)
    own = jnp.stack([tokens_in, cotangent]).reshape(-1, feats)
    own = jnp.dot(own, halves, preferred_element_type=jnp.float32).astype(jnp.bfloat16)
    columns = nz * tokens
    routes = micro * route_ids.shape[2]
    high = lax.reduce_precision(route_gates, 8, 7)
    meta = jnp.stack([route_ids.astype(jnp.float32), high, route_gates - high])
    meta = meta.transpose(0, 1, 3, 2).astype(jnp.bfloat16).reshape(3, routes, tokens)
    mine = jnp.arange(columns, dtype=jnp.int32) // tokens == z
    meta = jnp.where(mine, jnp.tile(meta, (1, 1, nz)), 0)
    meta = jnp.concatenate(
        [
            jnp.concatenate([meta[0], meta[1]], axis=1),
            jnp.concatenate([meta[2], jnp.zeros_like(meta[2])], axis=1),
        ]
    )
    meta = jnp.pad(meta, ((0, META_ROWS - 2 * routes), (0, feats - 2 * columns)))
    across = lax.ppermute(own, "xh", swap)
    weights = jnp.stack([gate_proj, up_proj, down_proj], axis=1)
    line = lax.all_gather(jnp.concatenate([own, across, meta]), "z", axis=0)
    weights = to_homes(weights)
    line_other = lax.ppermute(line, "c", swap)
    line_shape = (nz, 2, 2, micro, tokens, feats)

    expert_ids = jnp.stack(
        [((((xl + dx) % nxl) * ny + (y + dy) % ny) * nz + z) * 2 + core for dx, dy in steps]
    )
    copies = 1 + jnp.sum(
        (replica_plan[:, None, :] == expert_ids[None, :, None]).astype(jnp.int32), axis=2
    )
    all_ids = jnp.arange(expert_count, dtype=jnp.int32)
    limit = jnp.sum(
        jnp.where(all_ids[None, None, :] == expert_ids[None, :, None], capacity[:, None, :], 0),
        axis=2,
    )
    apart = jnp.arange(128, dtype=jnp.int32)
    divides = (apart % copies[:, :, None] == 0).astype(jnp.float32)
    limit = jnp.broadcast_to(limit[:, :, None].astype(jnp.float32), divides.shape)
    chunk_rows = micro * nz * SLOTS
    chunk = jax.ShapeDtypeStruct((2, 2, 2, chunk_rows, feats), jnp.bfloat16)
    chunk_pair = spec((2, 1, 2, chunk_rows, feats), lambda i, *refs: (0, i))
    pick_shape = (micro, offsets * nz * SLOTS, columns)
    pick = jax.ShapeDtypeStruct(pick_shape, jnp.bfloat16)
    line_rows = 2 * micro * tokens
    line_spec = spec((nz, line_rows, feats), lambda i, *refs: (0, i))
    sent = call(
        functools.partial(dispatch_kernel, offsets, tokens, route_ids.shape[2]),
        2,
        [spec(divides.shape), spec(limit.shape)]
        + [spec((nz, META_ROWS, feats), lambda i, *refs: (0, 2 * line_rows // META_ROWS))]
        + [line_spec] * 2,
        [spec(pick_shape)] * 3 + [chunk_pair] * offsets,
        [pick] * 3 + [chunk] * offsets,
    )(expert_ids, divides, limit, line, line, line_other)
    selections, sent = sent[:3], sent[3:]

    def moved(pieces, sign):
        done = [pieces[0]]
        for (dx, dy), piece in list(zip(steps, pieces))[1:]:
            pairs_list = [
                (a * ny + b, ((a + sign * dx) % nxl) * ny + (b + sign * dy) % ny)
                for a in range(nxl)
                for b in range(ny)
            ]
            done.append(lax.ppermute(piece, ("xl", "y"), pairs_list))
        return done

    arrived = moved(sent, 1)
    blk = jnp.arange(4, dtype=jnp.int32)
    quarters = (xh ^ (blk % 2)) * 2 + (core ^ (blk // 2))
    rows_all = offsets * chunk_rows
    blocks = expert_count // 8
    view = (4, blocks, 2)

    def early(i, *refs):
        i = jnp.minimum(i, 3)
        return (i // 2, i % 2)

    def late(i, *refs):
        i = jnp.maximum(i - 4, 0)
        return (i // 2, i % 2)

    stored = view + (3, pairs, width)
    results = call(
        functools.partial(expert_kernel, offsets),
        8,
        [spec((1,) + stored[1:], lambda i, q: (q[jnp.minimum(i, 3)],))]
        + [spec((1, 1, 2, chunk_rows, feats), early)] * offsets,
        [spec((1,) + stored[1:], lambda i, q: (q[jnp.maximum(i - 4, 0)],))]
        + [spec((1, 1, 2, chunk_rows, feats), late)] * offsets,
        [jax.ShapeDtypeStruct(stored, jnp.bfloat16)] + [chunk] * offsets,
        scratch=(
            pltpu.VMEM((3, 4, feats, width), jnp.bfloat16),
            pltpu.VMEM((4, 2, rows_all, feats), jnp.bfloat16),
            pltpu.VMEM((3, rows_all, width), jnp.float32),
            pltpu.VMEM((3, rows_all, width), jnp.bfloat16),
        ),
    )(quarters, weights.reshape(stored), *arrived)
    grads = to_homes(results[0].reshape(expert_count, 3, pairs, width))
    returned = moved(results[1:], -1)

    def combined(rc, *added):
        half = spec((nz, 1, 2, micro, tokens, feats), lambda i, *refs: (0, i))
        return call(
            functools.partial(combine_kernel, offsets),
            2,
            [spec(pick_shape)] * 3
            + [spec((1, 1, 2, chunk_rows, feats), lambda i, *refs: (rc, i))] * offsets
            + [half] * len(added),
            half,
            jax.ShapeDtypeStruct(line_shape, jnp.bfloat16),
        )(quarters, *selections, *returned, *added)

    keep = combined(0, lax.ppermute(combined(1), "c", swap))
    keep = lax.psum_scatter(keep.reshape(-1, feats), "z", scatter_dimension=0, tiled=True)
    keep = keep.reshape(2, -1, feats)
    total = keep[0].astype(jnp.float32) + lax.ppermute(keep[1], "xh", swap).astype(jnp.float32)
    total = jnp.dot(total.astype(jnp.bfloat16), halves.T, preferred_element_type=jnp.float32)
    total = total.astype(jnp.bfloat16).reshape(2, micro, tokens, feats)
    return (total[0], total[1], grads[:, 0], grads[:, 1], grads[:, 2])


def build(devices, sizes):
    mesh = Mesh(devices.reshape((2, 2) + sizes), DP + EXPERT)
    weight = P(None, EXPERT, DP)
    in_specs = (weight, P(None, EXPERT), P(None, EXPERT), weight, weight, weight, weight, P(), P())

    def step(*args):
        return shards(sizes, *args)

    return jax.shard_map(
        step,
        mesh=mesh,
        in_specs=in_specs,
        out_specs=(weight,) * 5,
        check_vma=False,
    )


def solution(mesh):
    sizes = (2, 4, 8)
    step = build(mesh.devices, sizes)
    return step
```

```python
import functools

import jax
import jax.numpy as jnp
from jax import lax
from jax.experimental import pallas as pl
from jax.experimental.pallas import tpu as pltpu
from jax.sharding import Mesh
from jax.sharding import PartitionSpec as P


INTERPRET = False
EXPERT = ("xl", "y", "z")
DP = ("xh", "c")
HOMES = ("xl", "y", "z", "c")
SLOTS = 4
META_ROWS = 32


def spec(shape, at=None):
    rank = len(shape)
    if at is None:
        return pl.BlockSpec(shape, lambda i, *refs: (0,) * rank)
    return pl.BlockSpec(shape, lambda i, *refs: (at(i, *refs) + (0,) * rank)[:rank])


def call(kernel, grid, in_specs, out_specs, out_shape, scratch=()):
    return pl.pallas_call(
        kernel,
        grid_spec=pltpu.PrefetchScalarGridSpec(
            num_scalar_prefetch=1,
            grid=(grid,),
            in_specs=in_specs,
            out_specs=out_specs,
            scratch_shapes=scratch,
        ),
        out_shape=out_shape,
        interpret=INTERPRET,
        compiler_params=pltpu.CompilerParams(
            dimension_semantics=("arbitrary",), vmem_limit_bytes=56 << 20
        ),
    )


def dot(a, b, a_dim, b_dim):
    return lax.dot_general(
        a, b, (((a_dim,), (b_dim,)), ((), ())), preferred_element_type=jnp.float32
    )


def select_rows(offsets, tokens, top, expert_ref, meta_ref, divides_ref, limit_ref, pick_refs):
    pick_ref, high_ref, low_ref = pick_refs
    micro = pick_ref.shape[0]
    rows = pick_ref.shape[1] // offsets
    columns = pick_ref.shape[2]
    named_rows = jnp.sum(meta_ref[...].astype(jnp.float32), axis=0)
    token = lax.broadcasted_iota(jnp.int32, (offsets, columns), 1) % tokens
    shape = (offsets * rows, columns)
    row = lax.broadcasted_iota(jnp.int32, shape, 0)
    source = lax.broadcasted_iota(jnp.int32, shape, 1) // tokens
    same = (row % rows) // SLOTS == source
    slot = (row % SLOTS).astype(jnp.float32)

    for m in range(micro):
        at = slice(m * top, (m + 1) * top)
        ids = named_rows[at, :columns]
        gates = (
            named_rows[at, columns : 2 * columns],
            named_rows[(micro + m) * top : (micro + m + 1) * top, :columns],
        )
        named, high, low = [], [], []
        for o in range(offsets):
            match = ids == expert_ref[o].astype(jnp.float32)
            named.append(jnp.sum(match.astype(jnp.float32), axis=0, keepdims=True))
            high.append(jnp.sum(jnp.where(match, gates[0], 0.0), axis=0, keepdims=True))
            low.append(jnp.sum(jnp.where(match, gates[1], 0.0), axis=0, keepdims=True))
        named = jnp.concatenate(named, axis=0)
        count = jnp.zeros_like(named)
        place = jnp.zeros_like(named)
        for apart in range(1, tokens):
            prior = jnp.where(token >= apart, pltpu.roll(named, apart, 1), 0.0)
            count += prior
            place += prior * divides_ref[m, :, apart : apart + 1]
        kept = (named > 0.0) & (place < limit_ref[m, :, :1])
        code = jnp.where(kept, count, -1.0)

        def spread(values):
            pieces = [jnp.broadcast_to(v, (rows, columns)) for v in values]
            return jnp.concatenate(pieces, axis=0)

        chosen = same & (spread([code[o : o + 1] for o in range(offsets)]) == slot)
        pick_ref[m] = jnp.where(chosen, 1.0, 0.0).astype(jnp.bfloat16)
        high_ref[m] = jnp.where(chosen, spread(high), 0.0).astype(jnp.bfloat16)
        low_ref[m] = jnp.where(chosen, spread(low), 0.0).astype(jnp.bfloat16)


def dispatch_kernel(
    offsets, tokens, top, expert_ref, divides_ref, limit_ref, meta_ref, own_ref, other_ref, *refs
):
    pick_refs, out_refs = refs[:3], refs[3:]
    pick_ref, high_ref, low_ref = pick_refs
    micro = pick_ref.shape[0]
    feats = own_ref.shape[2]
    rows = pick_ref.shape[1] // offsets

    @pl.when(pl.program_id(0) == 0)
    def _():
        select_rows(offsets, tokens, top, expert_ref, meta_ref, divides_ref, limit_ref, pick_refs)

    for m in range(micro):
        at = slice(m * rows, (m + 1) * rows)
        for rc, source in enumerate((own_ref, other_ref)):
            x = source[:, m * tokens : (m + 1) * tokens].reshape(-1, feats)
            g = source[:, (micro + m) * tokens : (micro + m + 1) * tokens].reshape(-1, feats)
            picked = dot(pick_ref[m], x, 1, 0).astype(jnp.bfloat16)
            scaled = dot(high_ref[m], g, 1, 0) + dot(low_ref[m], g, 1, 0)
            scaled = scaled.astype(jnp.bfloat16)
            for o in range(offsets):
                out_refs[o][rc, 0, 0, at] = picked[o * rows : (o + 1) * rows]
                out_refs[o][rc, 0, 1, at] = scaled[o * rows : (o + 1) * rows]


def combine_kernel(offsets, expert_ref, pick_ref, high_ref, low_ref, *refs):
    row_refs, refs = refs[:offsets], refs[offsets:]
    target, added = refs[-1], refs[:-1]
    micro = pick_ref.shape[0]
    rows = pick_ref.shape[1] // offsets
    shape = (target.shape[0],) + target.shape[4:]
    for m in range(micro):
        at = slice(m * rows, (m + 1) * rows)
        out = jnp.concatenate([r[0, 0, 0, at] for r in row_refs], axis=0)
        back = jnp.concatenate([r[0, 0, 1, at] for r in row_refs], axis=0)
        value = (dot(high_ref[m], out, 0, 0) + dot(low_ref[m], out, 0, 0)).reshape(shape)
        grad = dot(pick_ref[m], back, 0, 0).reshape(shape)
        for ref in added:
            value += ref[:, 0, 0, m].astype(jnp.float32)
            grad += ref[:, 0, 1, m].astype(jnp.float32)
        target[:, 0, 0, m] = value.astype(target.dtype)
        target[:, 0, 1, m] = grad.astype(target.dtype)


def swap_halves(lower, upper):
    half = lower.shape[1] // 2
    lane = lax.broadcasted_iota(jnp.int32, lower.shape, 1)
    first = jnp.where(lane < half, lower, pltpu.roll(upper, half, 1))
    second = jnp.where(lane < half, pltpu.roll(lower, half, 1), upper)
    return first, second


def expert_kernel(offsets, quarter_ref, fused_ref, down_ref, *refs):
    row_refs, refs = refs[:offsets], refs[offsets:]
    grad_ref, refs = refs[0], refs[1:]
    out_refs, (w_scr, row_scr, pre_scr, act_scr) = refs[:offsets], refs[offsets:]
    _, blocks, _, pairs, width = down_ref.shape
    depth = blocks * pairs
    rows = row_refs[0].shape[3]
    step = pl.program_id(0)

    @pl.when(step == 0)
    def _():
        pre_scr[...] = jnp.zeros_like(pre_scr)

    @pl.when(step < 4)
    def _():
        x = jnp.concatenate([r[0, 0, 0] for r in row_refs], axis=0)
        g = jnp.concatenate([r[0, 0, 1] for r in row_refs], axis=0)
        row_scr[step, 0] = x
        row_scr[step, 1] = g
        for k in range(3):
            if k < 2:
                lower, upper = fused_ref[0, :, 0, k], fused_ref[0, :, 1, k]
            else:
                lower, upper = down_ref[0, :, 0], down_ref[0, :, 1]
            halves = swap_halves(lower.reshape(depth, width), upper.reshape(depth, width))
            both = jnp.concatenate(halves, axis=0)
            w_scr[k, step] = both
            pre_scr[k] += dot(g if k == 2 else x, both, 1, 0)

    @pl.when(step == 3)
    def _():
        gate, up, hidden_grad = pre_scr[0], pre_scr[1], pre_scr[2]
        logistic = jax.nn.sigmoid(gate)
        swished = gate * logistic
        act_scr[2] = (swished * up).astype(jnp.bfloat16)
        act_scr[0] = (hidden_grad * up * logistic * (1.0 + gate * (1.0 - logistic))).astype(
            jnp.bfloat16
        )
        act_scr[1] = (hidden_grad * swished).astype(jnp.bfloat16)

    @pl.when(step >= 4)
    def _():
        blk = step - 4
        for k in range(3):
            total = dot(row_scr[blk, k // 2], act_scr[k], 0, 0).astype(jnp.bfloat16)
            lower, upper = swap_halves(total[:depth], total[depth:])
            grad_ref[0, :, 0, k] = lower.reshape(blocks, pairs, width)
            grad_ref[0, :, 1, k] = upper.reshape(blocks, pairs, width)
        out = dot(act_scr[2], w_scr[2, blk], 1, 1).astype(jnp.bfloat16)
        back = dot(act_scr[0], w_scr[0, blk], 1, 1)
        back = (back + dot(act_scr[1], w_scr[1, blk], 1, 1)).astype(jnp.bfloat16)
        for o in range(offsets):
            out_refs[o][0, 0, 0] = out[o * rows : (o + 1) * rows]
            out_refs[o][0, 0, 1] = back[o * rows : (o + 1) * rows]


def shards(
    sizes,
    tokens_in,
    route_ids,
    route_gates,
    cotangent,
    gate_proj,
    up_proj,
    down_proj,
    replica_plan,
    capacity,
):
    nxl, ny, nz = sizes
    micro, tokens, feats = tokens_in.shape
    expert_count, pairs, width = gate_proj.shape
    xh, core = lax.axis_index("xh"), lax.axis_index("c")
    xl, y, z = (lax.axis_index(name) for name in EXPERT)
    steps = [(dx, dy) for dx in range(nxl) for dy in range(ny)]
    steps = steps[:1] + sorted(steps[1:], key=lambda s: -s[0] - min(s[1], ny - s[1]))
    offsets = len(steps)
    swap = [(0, 1), (1, 0)]

    def to_homes(blocks):
        return lax.all_to_all(blocks, HOMES, split_axis=0, concat_axis=0, tiled=True)

    lane = jnp.arange(feats, dtype=jnp.int32)
    source = 2 * (lane % (feats // 2)) + lane // (feats // 2)
    halves = (lane[:, None] == source[None, :]).astype(jnp.bfloat16)
    own = jnp.stack([tokens_in, cotangent]).reshape(-1, feats)
    own = jnp.dot(own, halves, preferred_element_type=jnp.float32).astype(jnp.bfloat16)
    columns = nz * tokens
    routes = micro * route_ids.shape[2]
    high = lax.reduce_precision(route_gates, 8, 7)
    meta = jnp.stack([route_ids.astype(jnp.float32), high, route_gates - high])
    meta = meta.transpose(0, 1, 3, 2).astype(jnp.bfloat16).reshape(3, routes, tokens)
    mine = jnp.arange(columns, dtype=jnp.int32) // tokens == z
    meta = jnp.where(mine, jnp.tile(meta, (1, 1, nz)), 0)
    meta = jnp.concatenate(
        [
            jnp.concatenate([meta[0], meta[1]], axis=1),
            jnp.concatenate([meta[2], jnp.zeros_like(meta[2])], axis=1),
        ]
    )
    meta = jnp.pad(meta, ((0, META_ROWS - 2 * routes), (0, feats - 2 * columns)))
    across = lax.ppermute(own, "xh", swap)
    line = lax.all_gather(jnp.concatenate([own, across, meta]), "z", axis=0)
    down = to_homes(down_proj)
    fused = to_homes(jnp.stack([gate_proj, up_proj], axis=1))
    line_other = lax.ppermute(line, "c", swap)
    line_shape = (nz, 2, 2, micro, tokens, feats)

    expert_ids = jnp.stack(
        [((((xl + dx) % nxl) * ny + (y + dy) % ny) * nz + z) * 2 + core for dx, dy in steps]
    )
    copies = 1 + jnp.sum(
        (replica_plan[:, None, :] == expert_ids[None, :, None]).astype(jnp.int32), axis=2
    )
    all_ids = jnp.arange(expert_count, dtype=jnp.int32)
    limit = jnp.sum(
        jnp.where(all_ids[None, None, :] == expert_ids[None, :, None], capacity[:, None, :], 0),
        axis=2,
    )
    apart = jnp.arange(128, dtype=jnp.int32)
    divides = (apart % copies[:, :, None] == 0).astype(jnp.float32)
    limit = jnp.broadcast_to(limit[:, :, None].astype(jnp.float32), divides.shape)
    chunk_rows = micro * nz * SLOTS
    chunk = jax.ShapeDtypeStruct((2, 2, 2, chunk_rows, feats), jnp.bfloat16)
    chunk_pair = spec((2, 1, 2, chunk_rows, feats), lambda i, *refs: (0, i))
    pick_shape = (micro, offsets * nz * SLOTS, columns)
    pick = jax.ShapeDtypeStruct(pick_shape, jnp.bfloat16)
    line_rows = 2 * micro * tokens
    line_spec = spec((nz, line_rows, feats), lambda i, *refs: (0, i))
    sent = call(
        functools.partial(dispatch_kernel, offsets, tokens, route_ids.shape[2]),
        2,
        [spec(divides.shape), spec(limit.shape)]
        + [spec((nz, META_ROWS, feats), lambda i, *refs: (0, 2 * line_rows // META_ROWS))]
        + [line_spec] * 2,
        [spec(pick_shape)] * 3 + [chunk_pair] * offsets,
        [pick] * 3 + [chunk] * offsets,
    )(expert_ids, divides, limit, line, line, line_other)
    selections, sent = sent[:3], sent[3:]

    def moved(pieces, sign):
        done = [pieces[0]]
        for (dx, dy), piece in list(zip(steps, pieces))[1:]:
            pairs_list = [
                (a * ny + b, ((a + sign * dx) % nxl) * ny + (b + sign * dy) % ny)
                for a in range(nxl)
                for b in range(ny)
            ]
            done.append(lax.ppermute(piece, ("xl", "y"), pairs_list))
        return done

    arrived = moved(sent, 1)
    blk = jnp.arange(4, dtype=jnp.int32)
    quarters = (xh ^ (blk % 2)) * 2 + (core ^ (blk // 2))
    rows_all = offsets * chunk_rows
    blocks = expert_count // 8
    view = (4, blocks, 2)

    def early(i, *refs):
        i = jnp.minimum(i, 3)
        return (i // 2, i % 2)

    def late(i, *refs):
        i = jnp.maximum(i - 4, 0)
        return (i // 2, i % 2)

    stored = view + (3, pairs, width)
    results = call(
        functools.partial(expert_kernel, offsets),
        8,
        [
            spec((1, blocks, 2, 2, pairs, width), lambda i, q: (q[jnp.minimum(i, 3)],)),
            spec((1, blocks, 2, pairs, width), lambda i, q: (q[jnp.minimum(i, 3)],)),
        ]
        + [spec((1, 1, 2, chunk_rows, feats), early)] * offsets,
        [spec((1,) + stored[1:], lambda i, q: (q[jnp.maximum(i - 4, 0)],))]
        + [spec((1, 1, 2, chunk_rows, feats), late)] * offsets,
        [jax.ShapeDtypeStruct(stored, jnp.bfloat16)] + [chunk] * offsets,
        scratch=(
            pltpu.VMEM((3, 4, feats, width), jnp.bfloat16),
            pltpu.VMEM((4, 2, rows_all, feats), jnp.bfloat16),
            pltpu.VMEM((3, rows_all, width), jnp.float32),
            pltpu.VMEM((3, rows_all, width), jnp.bfloat16),
        ),
    )(
        quarters,
        fused.reshape(view + (2, pairs, width)),
        down.reshape(view + (pairs, width)),
        *arrived,
    )
    grads = to_homes(results[0].reshape(expert_count, 3, pairs, width))
    returned = moved(results[1:], -1)

    def combined(rc, *added):
        half = spec((nz, 1, 2, micro, tokens, feats), lambda i, *refs: (0, i))
        return call(
            functools.partial(combine_kernel, offsets),
            2,
            [spec(pick_shape)] * 3
            + [spec((1, 1, 2, chunk_rows, feats), lambda i, *refs: (rc, i))] * offsets
            + [half] * len(added),
            half,
            jax.ShapeDtypeStruct(line_shape, jnp.bfloat16),
        )(quarters, *selections, *returned, *added)

    keep = combined(0, lax.ppermute(combined(1), "c", swap))
    keep = lax.psum_scatter(keep.reshape(-1, feats), "z", scatter_dimension=0, tiled=True)
    keep = keep.reshape(2, -1, feats)
    across = lax.ppermute(keep[1], "xh", swap)
    gradients = tuple(grads[:, k] for k in range(3))
    total = keep[0].astype(jnp.float32) + across.astype(jnp.float32)
    total = jnp.dot(total.astype(jnp.bfloat16), halves.T, preferred_element_type=jnp.float32)
    total = total.astype(jnp.bfloat16).reshape(2, micro, tokens, feats)
    return (total[0], total[1], *gradients)


def build(devices, sizes):
    mesh = Mesh(devices.reshape((2, 2) + sizes), DP + EXPERT)
    weight = P(None, EXPERT, DP)
    in_specs = (weight, P(None, EXPERT), P(None, EXPERT), weight, weight, weight, weight, P(), P())

    def step(*args):
        return shards(sizes, *args)

    return jax.shard_map(
        step,
        mesh=mesh,
        in_specs=in_specs,
        out_specs=(weight,) * 5,
        check_vma=False,
    )


def solution(mesh):
    sizes = (2, 4, 8)
    step = build(mesh.devices, sizes)
    return step
```
